32 devices in a mesh: seq: 8 (over y, x, core), wshard: 4 (over z).
Axes of the slice: x: 2, y: 2, z: 4, core: 2. Of those that a mesh axis runs over, the one named last changes fastest.
Arguments:
- tokens: float32 [6144, 768], P(('seq', 'wshard')), may hold values from -18 to 18, as said below
- attention_norm_gain: float32 [2, 768], replicated, may hold values from 0.5 to 1.5
- qkv_weight: bfloat16 [2, 768, 2304], P(None, None, 'wshard'), may hold values from -7 to 7, as said below
- output_weight: bfloat16 [2, 768, 768], P(None, None, 'wshard'), may hold values from -0.75 to 0.75
- feedforward_norm_gain: float32 [2, 768], replicated, may hold values from 0.5 to 1.5
- input_weight: bfloat16 [2, 768, 2304], P(None, None, 'wshard'), may hold values from -0.21875 to 0.21875
- down_weight: bfloat16 [2, 1152, 768], P(None, 'wshard'), may hold values from -0.1875 to 0.1875
- cotangent: float32 [6144, 768], P(('seq', 'wshard')), may hold values from -18 to 18
Outputs:
- outputs: float32 [6144, 768], P(('seq', 'wshard'))
- input_grad: float32 [6144, 768], P(('seq', 'wshard'))
- grad_attention_gain: float32 [2, 768], replicated
- grad_qkv_weight: float32 [2, 768, 2304], P(None, 'seq', 'wshard')
- grad_output_weight: float32 [2, 768, 768], P(None, 'seq', 'wshard')
- grad_feedforward_gain: float32 [2, 768], replicated
- grad_input_weight: float32 [2, 768, 2304], P(None, 'seq', 'wshard')
- grad_down_weight: float32 [2, 1152, 768], P(None, 'wshard', 'seq')
The draws below stay inside these ranges and needn't reach their ends.
Inputs may be any that keep to these rules, and one draw needn't show every extreme that they name: `tokens`: activations of the first layer. `qkv_weight`: columns hold queries, keys, values, each head by head.
All inputs are finite; a program needn't handle non-finite values.
Results may differ from the reference program's by a relative error of at most 0.022.
Values may be sent and summed in bfloat16 or wider, within the bound.
A program may use at most 192 MiB of HBM per device.

```python
import math
from functools import partial
import jax
import jax.numpy as jnp
from jax import lax

D = 768
HEADS = 12
HDIM = 64
FF = 1152
WIN = 64
LAYERS = 2
SEQS = 1
TOK_DEV = 192
TOKENS = 6144


def draw_tokens(key, part):
    columns = jnp.exp(jax.random.uniform(jax.random.fold_in(key, 12), (1, D), jnp.float32, math.log(0.3), math.log(3.0)))
    noise = jnp.clip(jax.random.normal(jax.random.fold_in(key, 11), (TOKENS, D), jnp.float32), -6.0, 6.0)
    return (noise * columns).astype(jnp.float32)


def draw_cotangent(key, part):
    along = jnp.arange(TOKENS, dtype=jnp.float32) * (1.0 / TOKENS)
    noise = jnp.clip(jax.random.normal(jax.random.fold_in(key, 21), (TOKENS, D), jnp.float32), -6.0, 6.0)
    rising = jnp.exp(math.log(3.0) * along)[:, None]
    return (noise * rising).astype(jnp.float32)


def draw_qkv_weight(key, part):
    base = jnp.clip(jax.random.normal(jax.random.fold_in(key, 31), (LAYERS, D, 3 * D), jnp.float32), -6.0, 6.0) * D ** (-0.5)
    return base.astype(jnp.bfloat16)


def shard_levels(own_key, shape, shards, low, top_value):
    def one(axis_at, parts):
        heights = jax.random.uniform(jax.random.fold_in(jax.random.fold_in(own_key, 6), axis_at), (parts,), jnp.float32, low / len(shards), top_value / len(shards))
        return jnp.repeat(jnp.exp(heights), shape[axis_at] // parts).reshape((-1,) + (1,) * (len(shape) - axis_at - 1))

    loudness = one(*shards[0])
    for cut in shards[1:]:
        loudness = loudness * one(*cut)
    return loudness


def normal_values(rng, dims, spread, reach, shards=(), kind=jnp.bfloat16):
    gain = shard_levels(rng, dims, shards, -0.22, 0.18) if shards else 1.0
    values = jax.random.normal(rng, dims, jnp.float32) * spread * gain
    return jnp.minimum(jnp.maximum(values, -reach), reach).astype(kind)


def setup_inputs(seed: int = 0) -> dict:
    seeds = jax.random.split(jax.random.key(seed), 9)
    tokens = draw_tokens(jax.random.fold_in(seeds[8], 71), 0)
    attention_norm_gain = jnp.clip(1.0 + 0.1 * jax.random.normal(seeds[1], (LAYERS, D), jnp.float32), 0.5, 1.5)
    qkv_weight = draw_qkv_weight(jax.random.fold_in(seeds[8], 71), 0)
    output_weight = normal_values(seeds[3], (LAYERS, D, D), HDIM ** -0.5, 0.75, ((2, 4),))
    feedforward_norm_gain = jnp.clip(1.0 + 0.1 * jax.random.normal(seeds[4], (LAYERS, D), jnp.float32), 0.5, 1.5)
    input_weight = normal_values(seeds[5], (LAYERS, D, 2 * FF), D ** -0.5, 0.21875, ((2, 4),))
    down_weight = normal_values(seeds[6], (LAYERS, FF, D), FF ** -0.5, 0.1875, ((1, 4),))
    cotangent = draw_cotangent(jax.random.fold_in(seeds[8], 71), 0)
    return dict(tokens=tokens, attention_norm_gain=attention_norm_gain, qkv_weight=qkv_weight, output_weight=output_weight, feedforward_norm_gain=feedforward_norm_gain, input_weight=input_weight, down_weight=down_weight, cotangent=cotangent)


EPSILON = 1e-05
THETA = 10000.0

def rotate_half(values):
    middle_state = values.shape[-1] // 2
    return jnp.concatenate([-values[..., middle_state:], values[..., :middle_state]], axis=-1)

def rope_tables(positions):
    middle_state = HDIM // 2
    inverse = THETA ** (-(jnp.arange(middle_state, dtype=jnp.float32) * (2.0 / HDIM)))
    angles = positions.astype(jnp.float32)[:, None] * inverse[None, :]
    cosine = jnp.concatenate([jnp.cos(angles), jnp.cos(angles)], axis=1)
    sine = jnp.concatenate([jnp.sin(angles), jnp.sin(angles)], axis=1)
    return (cosine[:, None, :], sine[:, None, :])

def apply_rope(values, cosine, sine):
    return values * cosine + rotate_half(values) * sine

def undo_rope(grads, cosine, sine):
    return grads * cosine - rotate_half(grads * sine)

def layer_normalize(hidden_state):
    centred = hidden_state - lax.optimization_barrier(jnp.mean(hidden_state, axis=-1, keepdims=True))
    inverse = lax.rsqrt(lax.optimization_barrier(jnp.mean(centred * centred, axis=-1, keepdims=True)) + EPSILON)
    return (centred * inverse, inverse)

def norm_backward_step(normalized_gradient, normed, inverse, gain_row):
    scaled = normalized_gradient * gain_row
    result = scaled - lax.optimization_barrier(jnp.mean(scaled, axis=-1, keepdims=True)) - normed * lax.optimization_barrier(jnp.mean(scaled * normed, axis=-1, keepdims=True))
    return (result * inverse, lax.optimization_barrier(jnp.sum(normalized_gradient * normed, axis=0)))

def gelu_exact(inner_activation):
    return 0.5 * inner_activation * (1.0 + lax.erf(inner_activation * (1.0 / math.sqrt(2.0))))

def gelu_slope(inner_activation):
    return 0.5 * (1.0 + lax.erf(inner_activation * (1.0 / math.sqrt(2.0)))) + inner_activation * jnp.exp(-0.5 * inner_activation * inner_activation) * (1.0 / math.sqrt(2.0 * math.pi))

def band_mask(query_pos, key_pos, length):
    near = jnp.abs(query_pos[:, None] - key_pos[None, :]) <= WIN
    same = query_pos[:, None] // length == key_pos[None, :] // length
    return near & same

def block_scores(query_matrix, key_rows, allowed):
    scores = jnp.einsum('qhd,khd->hqk', query_matrix.astype(jnp.float32), key_rows.astype(jnp.float32)) * (1.0 / math.sqrt(HDIM))
    return jnp.where(allowed[None], scores, -1e+30)

def forward_block(query_matrix, padded_keys, padded_values, block, length, index):
    start = index * block
    query_rows = lax.dynamic_slice_in_dim(query_matrix, start, block, 0)
    key_rows = lax.dynamic_slice_in_dim(padded_keys, start, block + 2 * WIN, 0)
    value_rows = lax.dynamic_slice_in_dim(padded_values, start, block + 2 * WIN, 0)
    query_pos = start + jnp.arange(block, dtype=jnp.int32)
    key_pos = start - WIN + jnp.arange(block + 2 * WIN, dtype=jnp.int32)
    scores = block_scores(query_rows, key_rows, band_mask(query_pos, key_pos, length))
    top = lax.optimization_barrier(jnp.max(scores, axis=-1, keepdims=True))
    log_total = top + jnp.log(lax.optimization_barrier(jnp.sum(jnp.exp(scores - top), axis=-1, keepdims=True)))
    probs = jnp.exp(scores - log_total).astype(jnp.bfloat16)
    context_rows = jnp.einsum('hqk,khd->qhd', probs.astype(jnp.float32), value_rows.astype(jnp.float32)).astype(jnp.bfloat16)
    return (context_rows, log_total)

def back_block(query_matrix, padded_keys, padded_values, logsumexp_totals, grad_context, block, length, carry, index):
    grad_key_pad, grad_value_pad = carry
    start = index * block
    query_rows = lax.dynamic_slice_in_dim(query_matrix, start, block, 0)
    key_rows = lax.dynamic_slice_in_dim(padded_keys, start, block + 2 * WIN, 0)
    value_rows = lax.dynamic_slice_in_dim(padded_values, start, block + 2 * WIN, 0)
    grad_rows = lax.dynamic_slice_in_dim(grad_context, start, block, 0).astype(jnp.float32)
    query_pos = start + jnp.arange(block, dtype=jnp.int32)
    key_pos = start - WIN + jnp.arange(block + 2 * WIN, dtype=jnp.int32)
    scores = block_scores(query_rows, key_rows, band_mask(query_pos, key_pos, length))
    probs = jnp.exp(scores - logsumexp_totals[index])
    grad_values = jnp.einsum('hqk,qhd->khd', probs.astype(jnp.bfloat16).astype(jnp.float32), grad_rows)
    grad_probs = jnp.einsum('qhd,khd->hqk', grad_rows, value_rows.astype(jnp.float32))
    grad_scores = (probs * (grad_probs - lax.optimization_barrier(jnp.sum(probs * grad_probs, axis=-1, keepdims=True))) * (1.0 / math.sqrt(HDIM))).astype(jnp.bfloat16).astype(jnp.float32)
    grad_queries = jnp.einsum('hqk,khd->qhd', grad_scores, key_rows.astype(jnp.float32))
    grad_keys = jnp.einsum('hqk,qhd->khd', grad_scores, query_rows.astype(jnp.float32))
    old_keys = lax.dynamic_slice_in_dim(grad_key_pad, start, block + 2 * WIN, 0)
    old_values = lax.dynamic_slice_in_dim(grad_value_pad, start, block + 2 * WIN, 0)
    grad_key_pad = lax.dynamic_update_slice_in_dim(grad_key_pad, old_keys + grad_keys, start, 0)
    grad_value_pad = lax.dynamic_update_slice_in_dim(grad_value_pad, old_values + grad_values, start, 0)
    return ((grad_key_pad, grad_value_pad), grad_queries)

def reference(tokens, attention_norm_gain, qkv_weight, output_weight, feedforward_norm_gain, input_weight, down_weight, cotangent):
    length = TOKENS // SEQS
    positions = jnp.arange(TOKENS, dtype=jnp.int32)
    cosine, sine = rope_tables(positions % length)
    block = 512 if TOKENS % 512 == 0 else TOK_DEV
    count = TOKENS // block
    indices = jnp.arange(count, dtype=jnp.int32)
    scale_grad = 1.0 / math.sqrt(TOKENS)
    hidden_state = tokens
    saved_activations = []
    for layer_number in range(LAYERS):
        attention_standardized, attention_inverse_deviation = layer_normalize(hidden_state)
        attention_normalized = (attention_standardized * attention_norm_gain[layer_number]).astype(jnp.bfloat16)
        qkv = jnp.dot(attention_normalized, qkv_weight[layer_number], preferred_element_type=jnp.float32)
        query_matrix = apply_rope(qkv[:, :D].reshape(TOKENS, HEADS, HDIM), cosine, sine).astype(jnp.bfloat16)
        key_rows = apply_rope(qkv[:, D:2 * D].reshape(TOKENS, HEADS, HDIM), cosine, sine).astype(jnp.bfloat16)
        value_rows = qkv[:, 2 * D:].reshape(TOKENS, HEADS, HDIM).astype(jnp.bfloat16)
        padded_keys = jnp.pad(key_rows, ((WIN, WIN), (0, 0), (0, 0)))
        padded_values = jnp.pad(value_rows, ((WIN, WIN), (0, 0), (0, 0)))
        contexts, logsumexp_totals = lax.map(partial(forward_block, query_matrix, padded_keys, padded_values, block, length), indices)
        context_rows = contexts.reshape(TOKENS, D)
        middle_state = hidden_state + jnp.dot(context_rows, output_weight[layer_number], preferred_element_type=jnp.float32)
        feedforward_standardized, feedforward_inverse_deviation = layer_normalize(middle_state)
        feedforward_normalized = (feedforward_standardized * feedforward_norm_gain[layer_number]).astype(jnp.bfloat16)
        inner_activation = jnp.dot(feedforward_normalized, input_weight[layer_number], preferred_element_type=jnp.float32)
        gated_linear_output = (gelu_exact(inner_activation[:, :FF]) * inner_activation[:, FF:]).astype(jnp.bfloat16)
        saved_activations.append((attention_standardized, attention_inverse_deviation, attention_normalized, query_matrix, padded_keys, padded_values, logsumexp_totals, context_rows, feedforward_standardized, feedforward_inverse_deviation, feedforward_normalized, inner_activation, gated_linear_output))
        hidden_state = middle_state + jnp.dot(gated_linear_output, down_weight[layer_number], preferred_element_type=jnp.float32)
    outputs = hidden_state
    grad = cotangent
    list_again, list_qkv, list_out, list_fgain, list_in, list_down = ([], [], [], [], [], [])
    for layer_number in reversed(range(LAYERS)):
        attention_standardized, attention_inverse_deviation, attention_normalized, query_matrix, padded_keys, padded_values, logsumexp_totals, context_rows, feedforward_standardized, feedforward_inverse_deviation, feedforward_normalized, inner_activation, gated_linear_output = saved_activations[layer_number]
        grad_rounded = grad.astype(jnp.bfloat16)
        list_down.append(jnp.dot(gated_linear_output.T, grad_rounded, preferred_element_type=jnp.float32) * scale_grad)
        grad_geglu = jnp.dot(grad_rounded, down_weight[layer_number].T, preferred_element_type=jnp.float32)
        gate = inner_activation[:, :FF]
        upper = inner_activation[:, FF:]
        grad_inner = jnp.concatenate([grad_geglu * upper * gelu_slope(gate), grad_geglu * gelu_exact(gate)], axis=1).astype(jnp.bfloat16)
        list_in.append(jnp.dot(feedforward_normalized.T, grad_inner, preferred_element_type=jnp.float32) * scale_grad)
        normalized_gradient = jnp.dot(grad_inner, input_weight[layer_number].T, preferred_element_type=jnp.float32)
        partial_gradient, feedforward_gain_gradient = norm_backward_step(normalized_gradient, feedforward_standardized, feedforward_inverse_deviation, feedforward_norm_gain[layer_number])
        list_fgain.append(feedforward_gain_gradient * scale_grad)
        grad_middle = grad + partial_gradient
        grad_middle_rounded = grad_middle.astype(jnp.bfloat16)
        list_out.append(jnp.dot(context_rows.T, grad_middle_rounded, preferred_element_type=jnp.float32) * scale_grad)
        grad_context = jnp.dot(grad_middle_rounded, output_weight[layer_number].T, preferred_element_type=jnp.float32).astype(jnp.bfloat16).reshape(TOKENS, HEADS, HDIM)
        empty = jnp.zeros((TOKENS + 2 * WIN, HEADS, HDIM), jnp.float32)
        (grad_key_pad, grad_value_pad), grad_queries = lax.scan(partial(back_block, query_matrix, padded_keys, padded_values, logsumexp_totals, grad_context, block, length), (empty, empty), indices)
        grad_queries = grad_queries.reshape(TOKENS, HEADS, HDIM)
        grad_keys = grad_key_pad[WIN:WIN + TOKENS]
        grad_values = grad_value_pad[WIN:WIN + TOKENS]
        grad_qkv = jnp.concatenate([undo_rope(grad_queries, cosine, sine).reshape(TOKENS, D), undo_rope(grad_keys, cosine, sine).reshape(TOKENS, D), grad_values.reshape(TOKENS, D)], axis=1).astype(jnp.bfloat16)
        list_qkv.append(jnp.dot(attention_normalized.T, grad_qkv, preferred_element_type=jnp.float32) * scale_grad)
        attention_normalized_gradient = jnp.dot(grad_qkv, qkv_weight[layer_number].T, preferred_element_type=jnp.float32)
        attention_partial_gradient, attention_gain_gradient = norm_backward_step(attention_normalized_gradient, attention_standardized, attention_inverse_deviation, attention_norm_gain[layer_number])
        list_again.append(attention_gain_gradient * scale_grad)
        grad = grad_middle + attention_partial_gradient
    return (outputs, grad, jnp.stack(list_again[::-1]), jnp.stack(list_qkv[::-1]), jnp.stack(list_out[::-1]), jnp.stack(list_fgain[::-1]), jnp.stack(list_in[::-1]), jnp.stack(list_down[::-1]))
```

```python
import math

import jax
import jax.numpy as jnp
from jax import lax
from jax.sharding import PartitionSpec as P

D = 768
HEADS = 12
HDIM = 64
FF = 1152
WIN = 64
LAYERS = 2
SEQS = 1


EPSILON = 1e-05
THETA = 10000.0


def with_halo(cells, sides, width):
    for axis, dim in sides:
        count = lax.axis_size(axis)
        ends = count - 1
        head = lax.slice_in_dim(cells, 0, width, axis=dim)
        tail = lax.slice_in_dim(cells, cells.shape[dim] - width, cells.shape[dim], axis=dim)
        cells = jnp.concatenate(
            [
                lax.ppermute(tail, axis, [(i, (i + 1) % count) for i in range(ends)]),
                cells,
                lax.ppermute(head, axis, [((i + 1) % count, i) for i in range(ends)]),
            ],
            axis=dim,
        )
    return cells


def rotate_half(values):
    middle_state = values.shape[-1] // 2
    return jnp.concatenate([-values[..., middle_state:], values[..., :middle_state]], axis=-1)


def rope_tables(positions):
    middle_state = HDIM // 2
    inverse = THETA ** (-(jnp.arange(middle_state, dtype=jnp.float32) * (2.0 / HDIM)))
    angles = positions.astype(jnp.float32)[:, None] * inverse[None, :]
    cosine = jnp.concatenate([jnp.cos(angles), jnp.cos(angles)], axis=1)
    sine = jnp.concatenate([jnp.sin(angles), jnp.sin(angles)], axis=1)
    return (cosine[:, None, :], sine[:, None, :])


def apply_rope(values, cosine, sine):
    return values * cosine + rotate_half(values) * sine


def undo_rope(grads, cosine, sine):
    return grads * cosine - rotate_half(grads * sine)


def layer_normalize(hidden_state):
    centred = hidden_state - jnp.mean(hidden_state, axis=-1, keepdims=True)
    inverse = lax.rsqrt(jnp.mean(centred * centred, axis=-1, keepdims=True) + EPSILON)
    return (centred * inverse, inverse)


def norm_backward_step(normalized_gradient, normed, inverse, gain_row):
    scaled = normalized_gradient * gain_row
    result = (
        scaled
        - jnp.mean(scaled, axis=-1, keepdims=True)
        - normed * jnp.mean(scaled * normed, axis=-1, keepdims=True)
    )
    return (result * inverse, jnp.sum(normalized_gradient * normed, axis=0))


def gelu_exact(inner_activation):
    return 0.5 * inner_activation * (1.0 + lax.erf(inner_activation * (1.0 / math.sqrt(2.0))))


def gelu_slope(inner_activation):
    return 0.5 * (
        1.0 + lax.erf(inner_activation * (1.0 / math.sqrt(2.0)))
    ) + inner_activation * jnp.exp(-0.5 * inner_activation * inner_activation) * (
        1.0 / math.sqrt(2.0 * math.pi)
    )


def band_mask(query_pos, key_pos, length):
    near = jnp.abs(query_pos[:, None] - key_pos[None, :]) <= WIN
    same = query_pos[:, None] // length == key_pos[None, :] // length
    return near & same


def masked_scores(query_matrix, padded_keys, allowed):
    scores = jnp.einsum(
        "qhd,khd->hqk", query_matrix, padded_keys, preferred_element_type=jnp.float32
    ) * (1.0 / math.sqrt(HDIM))
    return jnp.where(allowed[None], scores, -1e30)


def attend_forward(query_matrix, padded_keys, padded_values, allowed):
    scores = masked_scores(query_matrix, padded_keys, allowed)
    top = jnp.max(scores, axis=-1, keepdims=True)
    log_total = top + jnp.log(jnp.sum(jnp.exp(scores - top), axis=-1, keepdims=True))
    probs = jnp.exp(scores - log_total).astype(jnp.bfloat16)
    context_rows = jnp.einsum(
        "hqk,khd->qhd", probs, padded_values, preferred_element_type=jnp.float32
    ).astype(jnp.bfloat16)
    return (context_rows, log_total)


def attend_backward(query_matrix, padded_keys, padded_values, allowed, log_total, grad_context):
    scores = masked_scores(query_matrix, padded_keys, allowed)
    probs = jnp.exp(scores - log_total)
    grad_values = jnp.einsum(
        "hqk,qhd->khd", probs.astype(jnp.bfloat16), grad_context, preferred_element_type=jnp.float32
    )
    grad_probs = jnp.einsum(
        "qhd,khd->hqk", grad_context, padded_values, preferred_element_type=jnp.float32
    )
    grad_scores = (
        probs
        * (grad_probs - jnp.sum(probs * grad_probs, axis=-1, keepdims=True))
        * (1.0 / math.sqrt(HDIM))
    ).astype(jnp.bfloat16)
    grad_queries = jnp.einsum(
        "hqk,khd->qhd", grad_scores, padded_keys, preferred_element_type=jnp.float32
    )
    grad_keys = jnp.einsum(
        "hqk,qhd->khd", grad_scores, query_matrix, preferred_element_type=jnp.float32
    )
    return (grad_queries, grad_keys, grad_values)


def gather_all(share, n_w, n_seq):
    whole = lax.all_gather(share, ("wshard", "seq"), axis=0, tiled=False)
    return whole.reshape(n_w, n_seq * share.shape[0], share.shape[1])


def sum_over_blocks(terms, n_w, n_seq):
    depth = terms.shape[1] // n_seq
    parts = terms.reshape(n_w, n_seq, depth, terms.shape[2]).transpose(1, 0, 2, 3)
    return lax.psum_scatter(parts, "seq", scatter_dimension=0, tiled=True)[0]


def sum_everywhere(values, axes):
    for axis in axes:
        count = lax.axis_size(axis)
        if count & (count - 1):
            values = lax.psum(values, axis)
            continue
        step = 1
        while step < count:
            pairs = [(i, i ^ step) for i in range(count)]
            values = values + lax.ppermute(values, axis, pairs)
            step *= 2
    return values


def per_device(
    tokens,
    attention_norm_gain,
    qkv_weight,
    output_weight,
    feedforward_norm_gain,
    input_weight,
    down_weight,
    cotangent,
):
    rows = tokens.shape[0]
    total_tokens = rows * lax.axis_size("seq") * lax.axis_size("wshard")
    length = total_tokens // SEQS
    block_index = lax.axis_index("seq") * lax.axis_size("wshard") + lax.axis_index("wshard")
    query_pos = block_index * rows + jnp.arange(rows, dtype=jnp.int32)
    key_pos = block_index * rows - WIN + jnp.arange(rows + 2 * WIN, dtype=jnp.int32)
    allowed = band_mask(query_pos, key_pos, length)
    cosine, sine = rope_tables(query_pos % length)
    scale_grad = 1.0 / math.sqrt(total_tokens)
    n_seq = lax.axis_size("seq")
    n_w = lax.axis_size("wshard")
    strip = D // n_seq
    seq_index = lax.axis_index("seq")
    col_qkv = qkv_weight.shape[2]
    col_out = output_weight.shape[2]
    col_in = input_weight.shape[2]
    row_down = down_weight.shape[1]

    def own_strip(weight, axis):
        return lax.dynamic_slice_in_dim(weight, seq_index * strip, strip, axis)

    gathered = []
    for layer_number in range(LAYERS):
        share = jnp.concatenate(
            [
                own_strip(qkv_weight[layer_number], 0),
                own_strip(input_weight[layer_number], 0),
                own_strip(down_weight[layer_number], 1).T,
                own_strip(output_weight[layer_number], 0),
            ],
            axis=1,
        )
        whole = gather_all(share, n_w, n_seq)
        ends = (col_qkv, col_qkv + col_in, col_qkv + col_in + row_down)
        gathered.append(
            (
                whole[:, :, : ends[0]],
                whole[:, :, ends[0] : ends[1]],
                whole[:, :, ends[1] : ends[2]],
                whole[:, :, ends[2] :],
            )
        )

    def columns_product(left, weight):
        return jnp.concatenate(
            [jnp.dot(left, weight[i], preferred_element_type=jnp.float32) for i in range(n_w)],
            axis=1,
        )

    def rows_product(left, weight):
        return jnp.einsum(
            "twf,wdf->td",
            left.reshape(rows, n_w, weight.shape[2]),
            weight,
            preferred_element_type=jnp.float32,
        )

    def blocks(left, right, width):
        return (
            jnp.einsum(
                "td,twf->wdf",
                left,
                right.reshape(rows, n_w, width),
                preferred_element_type=jnp.float32,
            )
            * scale_grad
        ).astype(jnp.bfloat16)

    hidden_state = tokens
    saved_activations = []
    for layer_number in range(LAYERS):
        full_qkv, full_in, full_down, full_out = gathered[layer_number]
        attention_standardized, attention_inverse_deviation = layer_normalize(hidden_state)
        attention_normalized = (attention_standardized * attention_norm_gain[layer_number]).astype(
            jnp.bfloat16
        )
        qkv = columns_product(attention_normalized, full_qkv)
        query_matrix = apply_rope(qkv[:, :D].reshape(rows, HEADS, HDIM), cosine, sine).astype(
            jnp.bfloat16
        )
        key_rows = (
            apply_rope(qkv[:, D : 2 * D].reshape(rows, HEADS, HDIM), cosine, sine)
            .astype(jnp.bfloat16)
            .reshape(rows, D)
        )
        value_rows = qkv[:, 2 * D :].astype(jnp.bfloat16)
        edged = with_halo(
            jnp.concatenate([key_rows, value_rows], axis=1), ((("seq", "wshard"), 0),), WIN
        )
        padded_keys = edged[:, :D].reshape(rows + 2 * WIN, HEADS, HDIM)
        padded_values = edged[:, D:].reshape(rows + 2 * WIN, HEADS, HDIM)
        context_rows, log_total = attend_forward(query_matrix, padded_keys, padded_values, allowed)
        context_rows = context_rows.reshape(rows, D)
        middle_state = hidden_state + columns_product(context_rows, full_out)
        feedforward_standardized, feedforward_inverse_deviation = layer_normalize(middle_state)
        feedforward_normalized = (
            feedforward_standardized * feedforward_norm_gain[layer_number]
        ).astype(jnp.bfloat16)
        inner_activation = columns_product(feedforward_normalized, full_in)
        gated_linear_output = (
            gelu_exact(inner_activation[:, :FF]) * inner_activation[:, FF:]
        ).astype(jnp.bfloat16)
        holding = None
        saved_activations.append(
            (
                holding,
                attention_standardized,
                attention_inverse_deviation,
                attention_normalized,
                query_matrix,
                padded_keys,
                padded_values,
                log_total,
                context_rows,
                feedforward_standardized,
                feedforward_inverse_deviation,
                feedforward_normalized,
                inner_activation,
                gated_linear_output,
            )
        )
        hidden_state = middle_state + rows_product(gated_linear_output, full_down)
    grad = cotangent
    list_again, list_fgain, block_sums = ([], [], [])
    for layer_number in reversed(range(LAYERS)):
        (
            holding,
            attention_standardized,
            attention_inverse_deviation,
            attention_normalized,
            query_matrix,
            padded_keys,
            padded_values,
            log_total,
            context_rows,
            feedforward_standardized,
            feedforward_inverse_deviation,
            feedforward_normalized,
            inner_activation,
            gated_linear_output,
        ) = saved_activations[layer_number]
        full_qkv, full_in, full_down, full_out = gathered[layer_number]
        grad_rounded = grad.astype(jnp.bfloat16)
        local_down = blocks(grad_rounded, gated_linear_output, row_down)
        grad_geglu = columns_product(grad_rounded, full_down)
        gate = inner_activation[:, :FF]
        upper = inner_activation[:, FF:]
        grad_inner = jnp.concatenate(
            [grad_geglu * upper * gelu_slope(gate), grad_geglu * gelu_exact(gate)], axis=1
        ).astype(jnp.bfloat16)
        local_in = blocks(feedforward_normalized, grad_inner, col_in)
        feed_terms = [local_in, local_down]
        if layer_number == 0:
            block_sums.append(
                sum_over_blocks(jnp.concatenate(feed_terms, axis=2), n_w, n_seq)
            )
            feed_terms = []
        normalized_gradient = rows_product(grad_inner, full_in)
        partial_gradient, feedforward_gain_gradient = norm_backward_step(
            normalized_gradient,
            feedforward_standardized,
            feedforward_inverse_deviation,
            feedforward_norm_gain[layer_number],
        )
        list_fgain.append(feedforward_gain_gradient * scale_grad)
        grad_middle = grad + partial_gradient
        grad_middle_rounded = grad_middle.astype(jnp.bfloat16)
        local_out = blocks(context_rows, grad_middle_rounded, col_out)
        grad_context = (
            rows_product(grad_middle_rounded, full_out)
            .astype(jnp.bfloat16)
            .reshape(rows, HEADS, HDIM)
        )
        grad_queries, grad_keys, grad_values = attend_backward(
            query_matrix, padded_keys, padded_values, allowed, log_total, grad_context
        )
        edge_terms = jnp.concatenate(
            [grad_keys.reshape(rows + 2 * WIN, D), grad_values.reshape(rows + 2 * WIN, D)], axis=1
        )
        rims = jnp.concatenate([edge_terms[:WIN], edge_terms[rows + WIN :]], axis=0)
        returned = with_halo(rims.astype(jnp.bfloat16), ((("seq", "wshard"), 0),), WIN).astype(
            rims.dtype
        )
        local_terms = edge_terms[WIN : WIN + rows]
        local_terms = (
            local_terms.at[:WIN].add(returned[:WIN]).at[rows - WIN :].add(returned[3 * WIN :])
        )
        grad_keys_local = local_terms[:, :D].reshape(rows, HEADS, HDIM)
        grad_qkv = jnp.concatenate(
            [
                undo_rope(grad_queries, cosine, sine).reshape(rows, D),
                undo_rope(grad_keys_local, cosine, sine).reshape(rows, D),
                local_terms[:, D:],
            ],
            axis=1,
        ).astype(jnp.bfloat16)
        local_qkv = blocks(attention_normalized, grad_qkv, col_qkv)
        block_sums.append(
            sum_over_blocks(
                jnp.concatenate(feed_terms + [local_qkv, local_out], axis=2), n_w, n_seq
            )
        )
        attention_normalized_gradient = rows_product(grad_qkv, full_qkv)
        attention_partial_gradient, attention_gain_gradient = norm_backward_step(
            attention_normalized_gradient,
            attention_standardized,
            attention_inverse_deviation,
            attention_norm_gain[layer_number],
        )
        list_again.append(attention_gain_gradient * scale_grad)
        grad = grad_middle + attention_partial_gradient
    gain_sums = sum_everywhere(
        jnp.concatenate([jnp.stack(list_again[::-1]), jnp.stack(list_fgain[::-1])], axis=0),
        ("seq", "wshard"),
    )
    summed = lax.psum_scatter(
        jnp.concatenate(block_sums, axis=2), "wshard", scatter_dimension=0, tiled=True
    )[0].astype(jnp.float32)
    per_layer = (col_in, row_down, col_qkv, col_out)
    pieces = []
    start = 0
    for width in per_layer * LAYERS:
        pieces.append(summed[:, start : start + width])
        start += width
    by_kind = [
        jnp.stack([pieces[4 * (LAYERS - 1 - n) + kind] for n in range(LAYERS)]) for kind in range(4)
    ]
    return (
        hidden_state,
        grad,
        gain_sums[:LAYERS],
        by_kind[2],
        by_kind[3],
        gain_sums[LAYERS:],
        by_kind[0],
        jnp.swapaxes(by_kind[1], 1, 2),
    )


def solution(mesh):
    placed = (
        P(("seq", "wshard"), None),
        P(),
        P(None, None, "wshard"),
        P(None, None, "wshard"),
        P(),
        P(None, None, "wshard"),
        P(None, "wshard", None),
        P(("seq", "wshard"), None),
    )
    return jax.shard_map(
        per_device,
        mesh=mesh,
        in_specs=placed,
        out_specs=(
            P(("seq", "wshard"), None),
            P(("seq", "wshard"), None),
            P(),
            P(None, "seq", "wshard"),
            P(None, "seq", "wshard"),
            P(),
            P(None, "seq", "wshard"),
            P(None, "wshard", "seq"),
        ),
        check_vma=False,
    )
```

```python
import math

import jax
import jax.numpy as jnp
from jax import lax
from jax.experimental import pallas as pl
from jax.experimental.pallas import tpu as pltpu
from jax.sharding import PartitionSpec as P

D = 768
HEADS = 12
HDIM = 64
FF = 1152
WIN = 64
LAYERS = 2
SEQS = 1


EPSILON = 1e-05
THETA = 10000.0


def with_halo(cells, sides, width):
    for axis, dim in sides:
        count = lax.axis_size(axis)
        ends = count - 1
        head = lax.slice_in_dim(cells, 0, width, axis=dim)
        tail = lax.slice_in_dim(cells, cells.shape[dim] - width, cells.shape[dim], axis=dim)
        cells = jnp.concatenate(
            [
                lax.ppermute(tail, axis, [(i, (i + 1) % count) for i in range(ends)]),
                cells,
                lax.ppermute(head, axis, [((i + 1) % count, i) for i in range(ends)]),
            ],
            axis=dim,
        )
    return cells


def rope_tables(positions):
    middle_state = HDIM // 2
    inverse = THETA ** (-(jnp.arange(middle_state, dtype=jnp.float32) * (2.0 / HDIM)))
    angles = positions.astype(jnp.float32)[:, None] * inverse[None, :]
    return (
        jnp.concatenate([jnp.cos(angles)] * 4, axis=1),
        jnp.concatenate([jnp.sin(angles)] * 4, axis=1),
    )


def layer_normalize(hidden_state):
    centred = hidden_state - jnp.mean(hidden_state, axis=-1, keepdims=True)
    inverse = lax.rsqrt(jnp.mean(centred * centred, axis=-1, keepdims=True) + EPSILON)
    return (centred * inverse, inverse)


def norm_backward_step(normalized_gradient, normed, inverse, gain_row):
    scaled = normalized_gradient * gain_row
    result = (
        scaled
        - jnp.mean(scaled, axis=-1, keepdims=True)
        - normed * jnp.mean(scaled * normed, axis=-1, keepdims=True)
    )
    return (result * inverse, jnp.sum(normalized_gradient * normed, axis=0))


def gelu_exact(inner_activation):
    return 0.5 * inner_activation * (1.0 + lax.erf(inner_activation * (1.0 / math.sqrt(2.0))))


def gelu_slope(inner_activation):
    return 0.5 * (
        1.0 + lax.erf(inner_activation * (1.0 / math.sqrt(2.0)))
    ) + inner_activation * jnp.exp(-0.5 * inner_activation * inner_activation) * (
        1.0 / math.sqrt(2.0 * math.pi)
    )


def lane_half(shape):
    return lax.rem(lax.broadcasted_iota(jnp.int32, shape, 1), HDIM) < HDIM // 2


def rotate_lanes(values, sign):
    width = values.shape[1]
    ahead = pltpu.roll(values, width - HDIM // 2, 1)
    behind = pltpu.roll(values, HDIM // 2, 1)
    return jnp.where(lane_half(values.shape), -sign * ahead, sign * behind)


def spread(table):
    return jnp.concatenate([table] * (D // table.shape[1]), axis=1)


def rope_kernel(qkv_ref, cosine_ref, sine_ref, query_ref, kv_ref):
    cosine = spread(cosine_ref[...])
    sine = spread(sine_ref[...])
    queries = qkv_ref[:, :D]
    keys = qkv_ref[:, D : 2 * D]
    query_ref[...] = (queries * cosine + rotate_lanes(queries, 1.0) * sine).astype(jnp.bfloat16)
    kv_ref[:, :D] = (keys * cosine + rotate_lanes(keys, 1.0) * sine).astype(jnp.bfloat16)
    kv_ref[:, D:] = qkv_ref[:, 2 * D :].astype(jnp.bfloat16)


def dot_f32(left, right, dims):
    return lax.dot_general(left, right, (dims, ((), ())), preferred_element_type=jnp.float32)


def head_scores(queries, keys, allowed):
    scores = dot_f32(queries, keys, ((1,), (1,))) * (1.0 / math.sqrt(HDIM))
    return jnp.where(allowed, scores, -1e30)


def window_mask(bounds_ref, rows):
    shape = (rows, rows + 2 * WIN)
    query = lax.broadcasted_iota(jnp.int32, shape, 0)
    key = lax.broadcasted_iota(jnp.int32, shape, 1)
    near = (key >= query) & (key <= query + 2 * WIN)
    return near & (key >= bounds_ref[0]) & (key < bounds_ref[1])


def forward_kernel(bounds_ref, query_ref, kv_ref, context_ref, log_ref):
    rows = query_ref.shape[0]
    allowed = window_mask(bounds_ref, rows)
    logs = []
    for head in range(HEADS):
        cols = slice(head * HDIM, (head + 1) * HDIM)
        shifted = slice(D + head * HDIM, D + (head + 1) * HDIM)
        scores = head_scores(query_ref[:, cols], kv_ref[:, cols], allowed)
        top = jnp.max(scores, axis=1, keepdims=True)
        log_total = top + jnp.log(jnp.sum(jnp.exp(scores - top), axis=1, keepdims=True))
        probs = jnp.exp(scores - log_total).astype(jnp.bfloat16)
        context_ref[:, cols] = dot_f32(probs, kv_ref[:, shifted], ((1,), (0,))).astype(
            jnp.bfloat16
        )
        logs.append(log_total)
    log_ref[...] = jnp.concatenate(logs, axis=1)


def backward_kernel(
    bounds_ref, query_ref, kv_ref, log_ref, grad_ref, dquery_ref, local_ref, rim_ref
):
    rows = query_ref.shape[0]
    allowed = window_mask(bounds_ref, rows)
    for head in range(HEADS):
        cols = slice(head * HDIM, (head + 1) * HDIM)
        shifted = slice(D + head * HDIM, D + (head + 1) * HDIM)
        queries = query_ref[:, cols]
        keys = kv_ref[:, cols]
        grads = grad_ref[:, cols]
        scores = head_scores(queries, keys, allowed)
        probs = jnp.exp(scores - log_ref[:, head : head + 1])
        grad_values = dot_f32(probs.astype(jnp.bfloat16), grads, ((0,), (0,)))
        grad_probs = dot_f32(grads, kv_ref[:, shifted], ((1,), (1,)))
        inner = jnp.sum(probs * grad_probs, axis=1, keepdims=True)
        grad_scores = (probs * (grad_probs - inner) * (1.0 / math.sqrt(HDIM))).astype(jnp.bfloat16)
        dquery_ref[:, cols] = dot_f32(grad_scores, keys, ((1,), (0,)))
        grad_keys = dot_f32(grad_scores, queries, ((0,), (0,)))
        for place, value in ((cols, grad_keys), (shifted, grad_values)):
            local_ref[:, place] = value[WIN : WIN + rows]
            rim_ref[:WIN, place] = value[:WIN].astype(jnp.bfloat16)
            rim_ref[WIN:, place] = value[WIN + rows :].astype(jnp.bfloat16)


def unrope_kernel(dquery_ref, local_ref, low_ref, high_ref, cosine_ref, sine_ref, out_ref):
    rows = dquery_ref.shape[0]
    cosine = spread(cosine_ref[...])
    sine = spread(sine_ref[...])
    queries = dquery_ref[...]
    out_ref[:, :D] = (queries * cosine - rotate_lanes(queries * sine, 1.0)).astype(jnp.bfloat16)
    local = local_ref[...]
    top = jnp.concatenate([low_ref[...].astype(jnp.float32), jnp.zeros((rows - WIN, 2 * D), jnp.float32)], axis=0)
    bottom = jnp.concatenate([jnp.zeros((rows - WIN, 2 * D), jnp.float32), high_ref[...].astype(jnp.float32)], axis=0)
    local = local + top + bottom
    keys = local[:, :D]
    out_ref[:, D : 2 * D] = (keys * cosine - rotate_lanes(keys * sine, 1.0)).astype(jnp.bfloat16)
    out_ref[:, 2 * D :] = local[:, D:].astype(jnp.bfloat16)


def local_call(kernel, outs, flops, operands, scalars=False):
    moved = sum(x.size * x.dtype.itemsize for x in operands) + sum(
        math.prod(shape) * jnp.dtype(kind).itemsize for shape, kind in outs
    )
    specs = [pl.BlockSpec(memory_space=pltpu.VMEM)] * len(operands)
    if scalars:
        specs[0] = pl.BlockSpec(memory_space=pltpu.SMEM)
    return pl.pallas_call(
        kernel,
        out_shape=[jax.ShapeDtypeStruct(shape, kind) for shape, kind in outs],
        in_specs=specs,
        out_specs=[pl.BlockSpec(memory_space=pltpu.VMEM)] * len(outs),
        cost_estimate=pl.CostEstimate(flops=flops, bytes_accessed=moved, transcendentals=0),
        compiler_params=pltpu.CompilerParams(vmem_limit_bytes=40 * 1024 * 1024),
    )(*operands)


def gather_all(share, n_w, n_seq):
    whole = lax.all_gather(share, ("wshard", "seq"), axis=0, tiled=False)
    return whole.reshape(n_w, n_seq * share.shape[0], share.shape[1])


def sum_over_blocks(terms, n_w, n_seq):
    depth = terms.shape[1] // n_seq
    parts = terms.reshape(n_w, n_seq, depth, terms.shape[2]).transpose(1, 0, 2, 3)
    parts = parts.reshape(n_seq * n_w, depth, terms.shape[2])
    return lax.psum_scatter(parts, "seq", scatter_dimension=0, tiled=True)


def sum_everywhere(values, axes):
    for axis in axes:
        count = lax.axis_size(axis)
        if count & (count - 1):
            values = lax.psum(values, axis)
            continue
        step = 1
        while step < count:
            pairs = [(i, i ^ step) for i in range(count)]
            values = values + lax.ppermute(values, axis, pairs)
            step *= 2
    return values


def per_device(
    tokens,
    attention_norm_gain,
    qkv_weight,
    output_weight,
    feedforward_norm_gain,
    input_weight,
    down_weight,
    cotangent,
):
    rows = tokens.shape[0]
    total_tokens = rows * lax.axis_size("seq") * lax.axis_size("wshard")
    length = total_tokens // SEQS
    block_index = lax.axis_index("seq") * lax.axis_size("wshard") + lax.axis_index("wshard")
    query_pos = block_index * rows + jnp.arange(rows, dtype=jnp.int32)
    begin = block_index * rows - WIN
    first = begin + WIN - (begin + WIN) % length
    bounds = jnp.stack([first - begin, first + length - begin]).astype(jnp.int32)
    cosine, sine = rope_tables(query_pos % length)
    scale_grad = 1.0 / math.sqrt(total_tokens)
    n_seq = lax.axis_size("seq")
    n_w = lax.axis_size("wshard")
    strip = D // n_seq
    seq_index = lax.axis_index("seq")
    col_qkv = qkv_weight.shape[2]
    col_out = output_weight.shape[2]
    col_in = input_weight.shape[2]
    row_down = down_weight.shape[1]

    def own_strip(weight, axis):
        return lax.dynamic_slice_in_dim(weight, seq_index * strip, strip, axis)

    gathered = []
    for layer_number in range(LAYERS):
        share = jnp.concatenate(
            [
                own_strip(qkv_weight[layer_number], 0),
                own_strip(input_weight[layer_number], 0),
                own_strip(down_weight[layer_number], 1).T,
                own_strip(output_weight[layer_number], 0),
            ],
            axis=1,
        )
        whole = gather_all(share, n_w, n_seq)
        ends = (col_qkv, col_qkv + col_in, col_qkv + col_in + row_down)
        gathered.append(
            (
                whole[:, :, : ends[0]],
                whole[:, :, ends[0] : ends[1]],
                whole[:, :, ends[1] : ends[2]],
                whole[:, :, ends[2] :],
            )
        )

    def columns_product(left, weight):
        return jnp.concatenate(
            [jnp.dot(left, weight[i], preferred_element_type=jnp.float32) for i in range(n_w)],
            axis=1,
        )

    def rows_product(left, weight):
        return jnp.einsum(
            "twf,wdf->td",
            left.reshape(rows, n_w, weight.shape[2]),
            weight,
            preferred_element_type=jnp.float32,
        )

    def blocks(left, right, width):
        return (
            jnp.einsum(
                "td,twf->wdf",
                left,
                right.reshape(rows, n_w, width),
                preferred_element_type=jnp.float32,
            )
            * scale_grad
        ).astype(jnp.bfloat16)

    hidden_state = tokens
    saved_activations = []
    for layer_number in range(LAYERS):
        full_qkv, full_in, full_down, full_out = gathered[layer_number]
        attention_standardized, attention_inverse_deviation = layer_normalize(hidden_state)
        attention_normalized = (attention_standardized * attention_norm_gain[layer_number]).astype(
            jnp.bfloat16
        )
        qkv = columns_product(attention_normalized, full_qkv)
        query_matrix, kv_rows = local_call(
            rope_kernel,
            [((rows, D), jnp.bfloat16), ((rows, 2 * D), jnp.bfloat16)],
            8 * rows * D,
            (qkv, cosine, sine),
        )
        padded = with_halo(kv_rows, ((("seq", "wshard"), 0),), WIN)
        context_rows, log_total = local_call(
            forward_kernel,
            [((rows, D), jnp.bfloat16), ((rows, HEADS), jnp.float32)],
            4 * rows * padded.shape[0] * D,
            (bounds, query_matrix, padded),
            True,
        )
        middle_state = hidden_state + columns_product(context_rows, full_out)
        feedforward_standardized, feedforward_inverse_deviation = layer_normalize(middle_state)
        feedforward_normalized = (
            feedforward_standardized * feedforward_norm_gain[layer_number]
        ).astype(jnp.bfloat16)
        inner_activation = columns_product(feedforward_normalized, full_in)
        gated_linear_output = (
            gelu_exact(inner_activation[:, :FF]) * inner_activation[:, FF:]
        ).astype(jnp.bfloat16)
        holding = None
        saved_activations.append(
            (
                holding,
                attention_standardized,
                attention_inverse_deviation,
                attention_normalized,
                query_matrix,
                padded,
                log_total,
                context_rows,
                feedforward_standardized,
                feedforward_inverse_deviation,
                feedforward_normalized,
                inner_activation,
                gated_linear_output,
            )
        )
        hidden_state = middle_state + rows_product(gated_linear_output, full_down)
    grad = cotangent
    list_again, list_fgain, block_sums = ([], [], [])
    for layer_number in reversed(range(LAYERS)):
        (
            holding,
            attention_standardized,
            attention_inverse_deviation,
            attention_normalized,
            query_matrix,
            padded,
            log_total,
            context_rows,
            feedforward_standardized,
            feedforward_inverse_deviation,
            feedforward_normalized,
            inner_activation,
            gated_linear_output,
        ) = saved_activations[layer_number]
        full_qkv, full_in, full_down, full_out = gathered[layer_number]
        grad_rounded = grad.astype(jnp.bfloat16)
        local_down = blocks(grad_rounded, gated_linear_output, row_down)
        grad_geglu = columns_product(grad_rounded, full_down)
        gate = inner_activation[:, :FF]
        upper = inner_activation[:, FF:]
        grad_inner = jnp.concatenate(
            [grad_geglu * upper * gelu_slope(gate), grad_geglu * gelu_exact(gate)], axis=1
        ).astype(jnp.bfloat16)
        local_in = blocks(feedforward_normalized, grad_inner, col_in)
        feed_terms = [local_in, local_down]
        if layer_number == 0:
            block_sums.append(
                sum_over_blocks(jnp.concatenate(feed_terms, axis=2), n_w, n_seq)
            )
            feed_terms = []
        normalized_gradient = rows_product(grad_inner, full_in)
        partial_gradient, feedforward_gain_gradient = norm_backward_step(
            normalized_gradient,
            feedforward_standardized,
            feedforward_inverse_deviation,
            feedforward_norm_gain[layer_number],
        )
        list_fgain.append(feedforward_gain_gradient * scale_grad)
        grad_middle = grad + partial_gradient
        grad_middle_rounded = grad_middle.astype(jnp.bfloat16)
        local_out = blocks(context_rows, grad_middle_rounded, col_out)
        grad_context = (
            rows_product(grad_middle_rounded, full_out).astype(jnp.bfloat16)
        )
        grad_queries, local_terms, rims = local_call(
            backward_kernel,
            [
                ((rows, D), jnp.float32),
                ((rows, 2 * D), jnp.float32),
                ((2 * WIN, 2 * D), jnp.bfloat16),
            ],
            10 * rows * padded.shape[0] * D,
            (bounds, query_matrix, padded, log_total, grad_context),
            True,
        )
        sites = ("seq", "wshard")
        count = lax.axis_size(sites)
        low = lax.ppermute(rims[WIN:], sites, [(i, i + 1) for i in range(count - 1)])
        high = lax.ppermute(rims[:WIN], sites, [(i + 1, i) for i in range(count - 1)])
        (grad_qkv,) = local_call(
            unrope_kernel,
            [((rows, 3 * D), jnp.bfloat16)],
            12 * rows * D,
            (grad_queries, local_terms, low, high, cosine, sine),
        )
        local_qkv = blocks(attention_normalized, grad_qkv, col_qkv)
        block_sums.append(
            sum_over_blocks(
                jnp.concatenate(feed_terms + [local_qkv, local_out], axis=2), n_w, n_seq
            )
        )
        attention_normalized_gradient = rows_product(grad_qkv, full_qkv)
        attention_partial_gradient, attention_gain_gradient = norm_backward_step(
            attention_normalized_gradient,
            attention_standardized,
            attention_inverse_deviation,
            attention_norm_gain[layer_number],
        )
        list_again.append(attention_gain_gradient * scale_grad)
        grad = grad_middle + attention_partial_gradient
    gain_sums = sum_everywhere(
        jnp.concatenate([jnp.stack(list_again[::-1]), jnp.stack(list_fgain[::-1])], axis=0),
        ("seq", "wshard"),
    )
    summed = lax.psum_scatter(
        jnp.concatenate(block_sums, axis=2), "wshard", scatter_dimension=0, tiled=True
    )[0].astype(jnp.float32)
    per_layer = (col_in, row_down, col_qkv, col_out)
    pieces = []
    start = 0
    for width in per_layer * LAYERS:
        pieces.append(summed[:, start : start + width])
        start += width
    by_kind = [
        jnp.stack([pieces[4 * (LAYERS - 1 - n) + kind] for n in range(LAYERS)]) for kind in range(4)
    ]
    return (
        hidden_state,
        grad,
        gain_sums[:LAYERS],
        by_kind[2],
        by_kind[3],
        gain_sums[LAYERS:],
        by_kind[0],
        jnp.swapaxes(by_kind[1], 1, 2),
    )


def solution(mesh):
    placed = (
        P(("seq", "wshard"), None),
        P(),
        P(None, None, "wshard"),
        P(None, None, "wshard"),
        P(),
        P(None, None, "wshard"),
        P(None, "wshard", None),
        P(("seq", "wshard"), None),
    )
    return jax.shard_map(
        per_device,
        mesh=mesh,
        in_specs=placed,
        out_specs=(
            P(("seq", "wshard"), None),
            P(("seq", "wshard"), None),
            P(),
            P(None, "seq", "wshard"),
            P(None, "seq", "wshard"),
            P(),
            P(None, "seq", "wshard"),
            P(None, "wshard", "seq"),
        ),
        check_vma=False,
    )
```
